32 devices in a mesh: row: 4 (over x, core), col: 8 (over z, y).
Axes of the slice: x: 2, y: 2, z: 4, core: 2. Of those that a mesh axis runs over, the one named last changes fastest.
Arguments:
- green_vectors: float32 [512, 131072], P('row', 'col'), may hold values from -6 to 6
- amplitudes: float32 [2048, 131072], P('row', 'col'), may hold values from -0.015625 to 0.015625
- cholesky: float32 [2048, 4096], P(('row', 'col')), may hold values from -0.125 to 0.125
Outputs:
- force_bias: float32 [512, 4096], P('col', 'row')
The draws below stay inside these ranges and needn't reach their ends.
All inputs are finite; a program needn't handle non-finite values.
Results may differ from the reference program's by a relative error of at most 0.000084.
Values sent between devices are 32-bit elements; how exact they have to be, the bound alone decides.
A program may use at most 128 MiB of HBM per device.

```python
import jax
import jax.numpy as jnp
from jax import lax

NCHOL = 4096
WALKERS = 512
PAIRS = 131072
SLAB = 2048


def level_of(rng, shape, shards, low, largest):
    def one(position, parts):
        heights = jax.random.uniform(jax.random.fold_in(jax.random.fold_in(rng, 6), position), (parts,), jnp.float32, low / len(shards), largest / len(shards))
        return jnp.repeat(jnp.exp(heights), shape[position] // parts).reshape((-1,) + (1,) * (len(shape) - position - 1))

    factor_of = one(*shards[0])
    for cut in shards[1:]:
        factor_of = factor_of * one(*cut)
    return factor_of


def noise(rng, dims, width, bound, shards=(), dtype=jnp.bfloat16):
    result = width * jax.random.normal(rng, dims, jnp.float32)
    if shards:
        result = result * level_of(rng, dims, shards, -0.22, 0.18)
    return jnp.clip(result, -bound, bound).astype(dtype)


def setup_inputs(seed: int = 0) -> dict:
    arg_keys = jax.random.split(jax.random.key(seed), 4)
    green_vectors = noise(arg_keys[0], (WALKERS, PAIRS), 1.0, 6.0, ((0, 4), (1, 8)), jnp.float32)
    amplitudes = noise(arg_keys[1], (SLAB, PAIRS), PAIRS ** -0.5, 0.015625, ((0, 4), (1, 8)), jnp.float32)
    cholesky = noise(arg_keys[2], (SLAB, NCHOL), SLAB ** -0.5, 0.125, ((0, 32),), jnp.float32)
    return dict(green_vectors=green_vectors, amplitudes=amplitudes, cholesky=cholesky)


def reference(green_vectors, amplitudes, cholesky):
    effective = lax.dot_general(green_vectors, amplitudes, (((1,), (1,)), ((), ())), precision=lax.Precision.HIGHEST, preferred_element_type=jnp.float32)
    return jnp.dot(effective, cholesky, precision=lax.Precision.HIGHEST, preferred_element_type=jnp.float32)
```

```python
import functools

import jax
import jax.numpy as jnp
from jax import lax
from jax.experimental import pallas as pl
from jax.experimental.pallas import tpu as pltpu
from jax.sharding import PartitionSpec as P

MESH = pl.DeviceIdType.MESH
F32, BF16 = jnp.float32, jnp.bfloat16
ROWS = 8
SLOTS = 4
CHUNK = 2048
TILE = 512


def halves(x):
    high = x.astype(BF16)
    return high, (x - high.astype(F32)).astype(BF16)


def dot_nt(left, right):
    return lax.dot_general(left, right, (((1,), (1,)), ((), ())), preferred_element_type=F32)


def dot_nn(left, right):
    return jnp.dot(left, right, preferred_element_type=F32)


def kernel(
    rows, cols, g, a, c, out, near, cbuf,
    ahi, alo, chi, clo, xs, ss, at, gt, ct, eown, acc, acc2, stage, eland, esend, esib, fbs, fbl,
    x_send, x_recv, f_send, f_recv, x_free, s_free, n_send, n_recv, ld,
    cl_sem, cs_send, cs_recv, c_send, c_recv, r_send, r_recv, ct_sem,
    e_send, e_recv, es_send, es_recv, fb_send, fb_recv,
):
    row, col = lax.axis_index("row"), lax.axis_index("col")
    sib = row + 1 - 2 * lax.rem(row, 2)
    far = lax.rem(row + rows // 2, rows)
    far_sib = lax.rem(sib + rows // 2, rows)
    pal = col + 1 - 2 * lax.rem(col, 2)
    opr, ng, _, pairs = g.shape
    depth = a.shape[0]
    held, wpo = opr * ng * ROWS, ng * ROWS
    chunk, nkc = ahi.shape[2], ahi.shape[0]
    tile = at.shape[2]
    per = chunk // tile
    cr, quarter = c.shape[0], c.shape[1] // rows
    npeer = cols // 2
    slots = xs.shape[0]
    n = 2 * opr * ROWS

    def remote(src, dst, send, recv, target):
        return pltpu.make_async_remote_copy(
            src_ref=src, dst_ref=dst, send_sem=send, recv_sem=recv, device_id=target, device_id_type=MESH
        )

    def loop(lo, hi, body):
        def step(i, carry):
            body(i)
            return carry

        lax.fori_loop(lo, hi, step, 0)

    barrier = pltpu.get_barrier_semaphore()
    pl.semaphore_signal(barrier, inc=1, device_id=(far, col), device_id_type=MESH)
    pl.semaphore_signal(barrier, inc=1, device_id=(sib, col), device_id_type=MESH)

    @functools.partial(loop, 1, cols)
    def _(t):
        pl.semaphore_signal(barrier, inc=1, device_id=(row, lax.rem(col + t, cols)), device_id_type=MESH)

    def load(i, slot):
        at_pairs = pl.ds(pl.multiple_of(i * tile, tile), tile)
        return [
            pltpu.make_async_copy(a.at[:, at_pairs], at.at[slot], ld.at[slot, 0]),
            pltpu.make_async_copy(g.at[:, :, :, at_pairs], gt.at[slot, 0], ld.at[slot, 1]),
            pltpu.make_async_copy(near.at[:, :, :, at_pairs], gt.at[slot, 1], ld.at[slot, 2]),
        ]

    for copy in load(0, 0)[:2]:
        copy.start()
    local = [
        pltpu.make_async_copy(
            c.at[:, pl.ds(pl.multiple_of(quarter_of * quarter, quarter), quarter)], cbuf.at[col, 0, h], cl_sem.at[h]
        )
        for h, quarter_of in enumerate((far, row))
    ]
    pl.semaphore_wait(barrier, cols + 1)

    def pairs_of(k):
        return pl.ds(pl.multiple_of(k * chunk, chunk), chunk)

    def x_copy(j, k):
        slot = lax.rem(j, slots)
        return remote(
            g.at[:, j, :, pairs_of(k)], xs.at[slot, :, :, pairs_of(k)],
            x_send.at[slot, k], x_recv.at[slot, k], (far, col),
        )

    def f_copy(j, k):
        slot = lax.rem(j, slots)
        return remote(
            xs.at[slot, :, :, pairs_of(k)], ss.at[slot, :, :, pairs_of(k)],
            f_send.at[slot, k], f_recv.at[slot, k], (sib, col),
        )

    def n_copy(k):
        return remote(g.at[:, :, :, pairs_of(k)], near.at[:, :, :, pairs_of(k)], n_send.at[k], n_recv.at[k], (sib, col))

    loop(0, nkc, lambda k: x_copy(0, k).start())
    n_copy(0).start()

    def c_quarter(m):
        return c.at[:, pl.ds(pl.multiple_of(m * quarter, quarter), quarter)]

    to_sib = [
        remote(c_quarter(m), cbuf.at[col, 1, h], cs_send.at[h], cs_recv.at[h], (sib, col))
        for h, m in enumerate((far_sib, sib))
    ]

    def c_target(p):
        return jnp.where(p == 0, pal, lax.rem(col + 2 * p, cols))

    def c_source(p):
        return jnp.where(p == 0, pal, lax.rem(col + cols - 2 * p, cols))

    def c_copies(p):
        target = (row, c_target(p))
        return [
            remote(c_quarter(far), cbuf.at[col, 0, 0], c_send.at[p, 0], c_recv.at[p, 0], target),
            remote(c_quarter(row), cbuf.at[col, 0, 1], c_send.at[p, 1], c_recv.at[p, 1], target),
            remote(cbuf.at[col, 1], cbuf.at[col, 1], c_send.at[p, 2], c_recv.at[p, 2], target),
        ]

    def r_copy(p):
        return remote(cbuf.at[c_source(p)], cbuf.at[c_source(p)], r_send.at[p], r_recv.at[p], (row, pal))

    for copy in to_sib:
        copy.start()
    loop(1, nkc, lambda k: n_copy(k).start())

    def send_own(p):
        for copy in c_copies(p)[:2]:
            copy.start()

    loop(0, npeer, send_own)
    for copy in local:
        copy.start()
    for j in range(1, min(slots, ng)):
        loop(0, nkc, functools.partial(lambda j, k: x_copy(j, k).start(), j))
    for copy in to_sib:
        copy.wait_recv()
    loop(0, npeer, lambda p: c_copies(p)[2].start())

    def relay(p):
        for copy in c_copies(p):
            copy.wait_recv()
        r_copy(p).start()

    eown[...] = jnp.zeros_like(eown)
    n_copy(0).wait_recv()
    load(0, 0)[2].start()

    @functools.partial(loop, 0, nkc)
    def _(kk):
        for q in range(per):
            slot = q % 2
            i = kk * per + q
            if q + 1 < per:
                for copy in load(i + 1, 1 - slot):
                    copy.start()
            else:

                @pl.when(kk + 1 < nkc)
                def _():
                    n_copy(kk + 1).wait_recv()
                    for copy in load(i + 1, 1 - slot):
                        copy.start()

            for copy in load(i, slot):
                copy.wait()
            high, low = halves(at[slot])
            ahi[kk, :, q * tile : (q + 1) * tile] = high
            alo[kk, :, q * tile : (q + 1) * tile] = low
            g_high, g_low = halves(gt[slot].reshape(2 * held, tile))
            pair = dot_nt(jnp.concatenate([g_high, g_low], axis=0), high)
            eown[...] += pair[: 2 * held] + (pair[2 * held :] + dot_nt(g_high, low))

    def steps(j, lo, hi):
        slot = lax.rem(j, slots)

        @functools.partial(loop, lo, hi)
        def _(k):
            @pl.when(k < nkc)
            def _():
                x_copy(j, k).wait_recv()
                f_copy(j, k).start()

            @pl.when(k > 0)
            def _():
                f_copy(j, k - 1).wait_recv()
                here = pairs_of(k - 1)
                block = jnp.concatenate(
                    [
                        xs[slot, :, :, here].reshape(n // 2, chunk),
                        ss[slot, :, :, here].reshape(n // 2, chunk),
                    ],
                    axis=0,
                )
                high, low = halves(block)
                acc[...] += dot_nt(jnp.concatenate([high, low], axis=0), ahi[k - 1])
                acc2[...] += dot_nt(high, alo[k - 1])

    def clear():
        acc[...] = jnp.zeros_like(acc)
        acc2[...] = jnp.zeros_like(acc2)

    def e_copy(j, t):
        target = lax.rem(col + t, cols)
        return remote(stage.at[j, target], eland.at[j, t], e_send.at[j, t], e_recv.at[j, t], (row, target))

    def es_copy(j):
        return remote(esend.at[j], esib.at[j], es_send.at[j], es_recv.at[j], (sib, col))

    def scatter(j):
        for i in range(opr):
            mine = pl.multiple_of(i * wpo + j * ROWS, ROWS)
            stage[j, row * opr + i] = eown[pl.ds(mine, ROWS)]
            stage[j, sib * opr + i] = eown[pl.ds(held + mine, ROWS)]
            at_far, at_sib = slice(i * ROWS, (i + 1) * ROWS), slice((opr + i) * ROWS, (opr + i + 1) * ROWS)
            for owner, here in ((far, at_far), (far_sib, at_sib)):
                below = slice(n + here.start, n + here.stop)
                stage[j, owner * opr + i] = acc[here] + (acc[below] + acc2[here])
        loop(1, cols, lambda t: e_copy(j, t).start())

    def gather(j):
        def add(t, total):
            e_copy(j, t).wait_recv()
            return total + eland[j, t]

        esend[j] = lax.fori_loop(1, cols, add, stage[j, col])
        es_copy(j).start()

    def fb_copy(first, last):
        return remote(
            fbs.at[pl.ds(first, last - first)], fbl.at[pl.ds(first, last - first)],
            fb_send.at[first], fb_recv.at[first], (far, col),
        )

    def bias(first, last):
        m = (last - first) * ROWS

        def part(ref):
            high, low = halves(ref[first:last].reshape(m, depth))
            return jnp.concatenate([high, low], axis=0), high

        def term(both, high, q, h):
            here = slice(h * quarter, (h + 1) * quarter)
            pair = dot_nn(both, chi[q, :, here])
            return pair[:m] + (pair[m:] + dot_nn(high, clo[q, :, here]))

        mine = part(esend)
        away = term(*mine, 0, 0)
        for j in range(first, last):
            es_copy(j).wait_recv()
        other = part(esib)
        fbs[first:last] = (away + term(*other, 1, 0)).reshape(last - first, ROWS, quarter)
        fb_copy(first, last).start()
        out[first * ROWS : last * ROWS] = term(*mine, 0, 1) + term(*other, 1, 1)

    def turn(j):
        clear()

        @pl.when(j >= slots)
        def _():
            pl.semaphore_wait(s_free, 1)

        steps(j, 0, nkc + 1)
        scatter(j)
        loop(0, nkc, lambda k: f_copy(j, k).wait_send())

        @pl.when(j + slots < ng)
        def _():
            pl.semaphore_signal(x_free, inc=1, device_id=(far, col), device_id_type=MESH)
            pl.semaphore_signal(s_free, inc=1, device_id=(sib, col), device_id_type=MESH)

        @pl.when((j >= 1) & (j + slots - 1 < ng))
        def _():
            pl.semaphore_wait(x_free, 1)

            def again(k):
                x_copy(j - 1, k).wait_send()
                x_copy(j + slots - 1, k).start()

            loop(0, nkc, again)

        @pl.when((j >= 3) & (j - 2 < npeer))
        def _():
            relay(j - 2)

        @pl.when(j >= 1)
        def _():
            gather(j - 1)

    last = ng - 1
    if last:
        loop(0, last, turn)
    loop(max(1, last - 2), npeer, relay)

    for copy in c_copies(0):
        copy.wait_recv()
    loop(1, npeer, lambda p: r_copy(p).wait_recv())
    for copy in local:
        copy.wait()
    block = ct.shape[1]

    def c_load(i, slot):
        return pltpu.make_async_copy(cbuf.at[pl.ds(i * block, block)], ct.at[slot], ct_sem.at[slot])

    c_load(0, 0).start()

    @functools.partial(loop, 0, cols // block)
    def _(i):
        slot = lax.rem(i, 2)

        @pl.when(i + 1 < cols // block)
        def _():
            c_load(i + 1, 1 - slot).start()

        c_load(i, slot).wait()
        here = pl.ds(pl.multiple_of(i * block * cr, block * cr), block * cr)
        for q in range(2):
            for h in range(2):
                high, low = halves(ct[slot, :, q, h].reshape(block * cr, quarter))
                chi[q, here, h * quarter : (h + 1) * quarter] = high
                clo[q, here, h * quarter : (h + 1) * quarter] = low

    batches = []
    if last > 1:
        bias(0, last - 1)
        batches.append((0, last - 1))
    clear()
    if last >= slots:
        pl.semaphore_wait(s_free, 1)
    middle = (nkc + 1) // 2
    steps(last, 0, middle)
    if last:
        gather(last - 1)
        bias(last - 1, last)
        batches.append((last - 1, last))
    steps(last, middle, nkc + 1)
    scatter(last)
    gather(last)
    bias(last, ng)
    batches.append((last, ng))
    for first, end in batches:
        fb_copy(first, end).wait_recv()
        out[first * ROWS : end * ROWS] += fbl[first:end].reshape((end - first) * ROWS, quarter)

    loop(0, nkc, lambda k: f_copy(last, k).wait_send())
    for j in range(max(0, ng - slots), ng):
        loop(0, nkc, functools.partial(lambda j, k: x_copy(j, k).wait_send(), j))
    loop(0, nkc, lambda k: n_copy(k).wait_send())
    for copy in to_sib:
        copy.wait_send()

    def sent(p):
        for copy in c_copies(p):
            copy.wait_send()

    loop(0, npeer, sent)
    loop(1, npeer, lambda p: r_copy(p).wait_send())

    def e_sent(j):
        loop(1, cols, lambda t: e_copy(j, t).wait_send())
        es_copy(j).wait_send()

    loop(0, ng, e_sent)
    for first, end in batches:
        fb_copy(first, end).wait_send()


def per_device(green_vectors, amplitudes, cholesky):
    rows, cols = lax.axis_size("row"), lax.axis_size("col")
    held, pairs = green_vectors.shape
    depth = amplitudes.shape[0]
    cr, quarter = cholesky.shape[0], cholesky.shape[1] // rows
    if rows != 4 or cols % 2 or rows * held % (cols * ROWS):
        raise ValueError("unexpected mesh")
    wpo = rows * held // cols
    opr, ng = held // wpo, wpo // ROWS
    chunk = min(CHUNK, pairs)
    nkc, nk = pairs // chunk, 2
    slots = min(SLOTS, ng)
    n = 2 * opr * ROWS
    block = max(1, 16 // cr)
    dma = pltpu.SemaphoreType.DMA
    vmem = pltpu.VMEM
    scratch = [
        vmem((nkc, depth, chunk), BF16),
        vmem((nkc, depth, chunk), BF16),
        vmem((2, cols * cr, 2 * quarter), BF16),
        vmem((2, cols * cr, 2 * quarter), BF16),
        vmem((slots, opr, ROWS, pairs), F32),
        vmem((slots, opr, ROWS, pairs), F32),
        vmem((2, depth, TILE), F32),
        vmem((2, 2, opr, ng, ROWS, TILE), F32),
        vmem((2, block, 2, 2, cr, quarter), F32),
        vmem((2 * held, depth), F32),
        vmem((2 * n, depth), F32),
        vmem((n, depth), F32),
        vmem((ng, cols, ROWS, depth), F32),
        vmem((ng, cols, ROWS, depth), F32),
        vmem((ng, ROWS, depth), F32),
        vmem((ng, ROWS, depth), F32),
        vmem((ng, ROWS, quarter), F32),
        vmem((ng, ROWS, quarter), F32),
        dma((slots, nkc)),
        dma((slots, nkc)),
        dma((slots, nkc)),
        dma((slots, nkc)),
        pltpu.SemaphoreType.REGULAR,
        pltpu.SemaphoreType.REGULAR,
        dma((nkc,)),
        dma((nkc,)),
        dma((2, 3)),
        dma((2,)),
        dma((2,)),
        dma((2,)),
        dma((cols // 2, 3)),
        dma((cols // 2, 3)),
        dma((cols // 2,)),
        dma((cols // 2,)),
        dma((2,)),
        dma((ng, cols)),
        dma((ng, cols)),
        dma((ng,)),
        dma((ng,)),
        dma((ng,)),
        dma((ng,)),
    ]
    hbm = pl.BlockSpec(memory_space=pl.ANY)
    return pl.pallas_call(
        functools.partial(kernel, rows, cols),
        out_shape=(
            jax.ShapeDtypeStruct((wpo, quarter), F32),
            jax.ShapeDtypeStruct((opr, ng, ROWS, pairs), F32),
            jax.ShapeDtypeStruct((cols, 2, 2, cr, quarter), F32),
        ),
        in_specs=[hbm] * 3,
        out_specs=(pl.BlockSpec(memory_space=pltpu.VMEM), hbm, hbm),
        scratch_shapes=scratch,
        compiler_params=pltpu.CompilerParams(
            collective_id=0, has_side_effects=True, vmem_limit_bytes=67_043_328
        ),
    )(green_vectors.reshape(opr, ng, ROWS, pairs), amplitudes, cholesky)[0]


def solution(mesh):
    placed = (P("row", "col"), P("row", "col"), P(("row", "col"), None))
    return jax.shard_map(
        per_device, mesh=mesh, in_specs=placed, out_specs=P("col", "row"), check_vma=False
    )
```

```python
import functools

import jax
import jax.numpy as jnp
from jax import lax
from jax.experimental import pallas as pl
from jax.experimental.pallas import tpu as pltpu
from jax.sharding import PartitionSpec as P

MESH = pl.DeviceIdType.MESH
F32, BF16 = jnp.float32, jnp.bfloat16
ROWS = 8
SLOTS = 4
CHUNK = 2048
TILE = 512
RELAYS = (1, 3)


def halves(x):
    high = x.astype(BF16)
    return high, (x - high.astype(F32)).astype(BF16)


def dot_nt(left, right):
    return lax.dot_general(left, right, (((1,), (1,)), ((), ())), preferred_element_type=F32)


def dot_nn(left, right):
    return jnp.dot(left, right, preferred_element_type=F32)


def kernel(
    rows, cols, g, a, c, out, near, cbuf,
    ahi, alo, chi, clo, xs, ss, at, gt, ct, eown, acc, acc2, stage, eland, esend, esib, fbs, fbl,
    x_send, x_recv, f_send, f_recv, x_free, s_free, n_send, n_recv, ld,
    cl_sem, cs_send, cs_recv, c_send, c_recv, r_send, r_recv, ct_sem,
    e_send, e_recv, es_send, es_recv, fb_send, fb_recv,
):
    row, col = lax.axis_index("row"), lax.axis_index("col")
    sib = row + 1 - 2 * lax.rem(row, 2)
    far = lax.rem(row + rows // 2, rows)
    far_sib = lax.rem(sib + rows // 2, rows)
    pal = col + 1 - 2 * lax.rem(col, 2)
    opr, ng, _, pairs = g.shape
    depth = a.shape[0]
    held, wpo = opr * ng * ROWS, ng * ROWS
    chunk, nkc = ahi.shape[2], ahi.shape[0]
    tile = at.shape[2]
    per = chunk // tile
    cr, quarter = c.shape[0], c.shape[1] // rows
    npeer = cols // 2
    slots = xs.shape[0]
    n = 2 * opr * ROWS

    def remote(src, dst, send, recv, target):
        return pltpu.make_async_remote_copy(
            src_ref=src, dst_ref=dst, send_sem=send, recv_sem=recv, device_id=target, device_id_type=MESH
        )

    def loop(lo, hi, body):
        def step(i, carry):
            body(i)
            return carry

        lax.fori_loop(lo, hi, step, 0)

    barrier = pltpu.get_barrier_semaphore()
    pl.semaphore_signal(barrier, inc=1, device_id=(far, col), device_id_type=MESH)
    pl.semaphore_signal(barrier, inc=1, device_id=(sib, col), device_id_type=MESH)

    @functools.partial(loop, 1, cols)
    def _(t):
        pl.semaphore_signal(barrier, inc=1, device_id=(row, lax.rem(col + t, cols)), device_id_type=MESH)

    def load(i, slot):
        at_pairs = pl.ds(pl.multiple_of(i * tile, tile), tile)
        return [
            pltpu.make_async_copy(a.at[:, at_pairs], at.at[slot], ld.at[slot, 0]),
            pltpu.make_async_copy(g.at[:, :, :, at_pairs], gt.at[slot, 0], ld.at[slot, 1]),
            pltpu.make_async_copy(near.at[:, :, :, at_pairs], gt.at[slot, 1], ld.at[slot, 2]),
        ]

    for copy in load(0, 0)[:2]:
        copy.start()
    local = [
        pltpu.make_async_copy(
            c.at[:, pl.ds(pl.multiple_of(quarter_of * quarter, quarter), quarter)], cbuf.at[col, 0, h], cl_sem.at[h]
        )
        for h, quarter_of in enumerate((far, row))
    ]
    pl.semaphore_wait(barrier, cols + 1)

    def pairs_of(k):
        return pl.ds(pl.multiple_of(k * chunk, chunk), chunk)

    def x_copy(j, k):
        slot = lax.rem(j, slots)
        return remote(
            g.at[:, j, :, pairs_of(k)], xs.at[slot, :, :, pairs_of(k)],
            x_send.at[slot, k], x_recv.at[slot, k], (far, col),
        )

    def f_copy(j, k):
        slot = lax.rem(j, slots)
        return remote(
            xs.at[slot, :, :, pairs_of(k)], ss.at[slot, :, :, pairs_of(k)],
            f_send.at[slot, k], f_recv.at[slot, k], (sib, col),
        )

    def n_copy(k):
        return remote(g.at[:, :, :, pairs_of(k)], near.at[:, :, :, pairs_of(k)], n_send.at[k], n_recv.at[k], (sib, col))

    loop(0, nkc, lambda k: x_copy(0, k).start())
    n_copy(0).start()

    def c_quarter(m):
        return c.at[:, pl.ds(pl.multiple_of(m * quarter, quarter), quarter)]

    to_sib = [
        remote(c_quarter(m), cbuf.at[col, 1, h], cs_send.at[h], cs_recv.at[h], (sib, col))
        for h, m in enumerate((far_sib, sib))
    ]

    def c_target(p):
        return jnp.where(p == 0, pal, lax.rem(col + 2 * p, cols))

    def c_source(p):
        return jnp.where(p == 0, pal, lax.rem(col + cols - 2 * p, cols))

    def c_copies(p):
        target = (row, c_target(p))
        return [
            remote(c_quarter(far), cbuf.at[col, 0, 0], c_send.at[p, 0], c_recv.at[p, 0], target),
            remote(c_quarter(row), cbuf.at[col, 0, 1], c_send.at[p, 1], c_recv.at[p, 1], target),
            remote(cbuf.at[col, 1], cbuf.at[col, 1], c_send.at[p, 2], c_recv.at[p, 2], target),
        ]

    def r_copy(p, q):
        piece = cbuf.at[c_source(p), q]
        return remote(piece, piece, r_send.at[p, q], r_recv.at[p, q], (row, pal))

    for copy in to_sib:
        copy.start()
    loop(1, nkc, lambda k: n_copy(k).start())

    def send_own(p):
        for copy in c_copies(p)[:2]:
            copy.start()

    loop(0, npeer, send_own)
    for copy in local:
        copy.start()
    for j in range(1, min(slots, ng)):
        loop(0, nkc, functools.partial(lambda j, k: x_copy(j, k).start(), j))
    for copy in to_sib:
        copy.wait_recv()
    loop(0, npeer, lambda p: c_copies(p)[2].start())

    def relay(q):
        def one(p):
            copies = c_copies(p)
            for copy in copies[2:] if q else copies[:2]:
                copy.wait_recv()
            r_copy(p, q).start()

        loop(1, npeer, one)

    eown[...] = jnp.zeros_like(eown)
    n_copy(0).wait_recv()
    load(0, 0)[2].start()

    @functools.partial(loop, 0, nkc)
    def _(kk):
        for q in range(per):
            slot = q % 2
            i = kk * per + q
            if q + 1 < per:
                for copy in load(i + 1, 1 - slot):
                    copy.start()
            else:

                @pl.when(kk + 1 < nkc)
                def _():
                    n_copy(kk + 1).wait_recv()
                    for copy in load(i + 1, 1 - slot):
                        copy.start()

            for copy in load(i, slot):
                copy.wait()
            high, low = halves(at[slot])
            ahi[kk, :, q * tile : (q + 1) * tile] = high
            alo[kk, :, q * tile : (q + 1) * tile] = low
            g_high, g_low = halves(gt[slot].reshape(2 * held, tile))
            pair = dot_nt(jnp.concatenate([g_high, g_low], axis=0), high)
            eown[...] += pair[: 2 * held] + (pair[2 * held :] + dot_nt(g_high, low))

    def steps(j, lo, hi):
        slot = lax.rem(j, slots)

        @functools.partial(loop, lo, hi)
        def _(k):
            @pl.when(k < nkc)
            def _():
                x_copy(j, k).wait_recv()
                f_copy(j, k).start()

            @pl.when(k > 0)
            def _():
                f_copy(j, k - 1).wait_recv()
                here = pairs_of(k - 1)
                block = jnp.concatenate(
                    [
                        xs[slot, :, :, here].reshape(n // 2, chunk),
                        ss[slot, :, :, here].reshape(n // 2, chunk),
                    ],
                    axis=0,
                )
                high, low = halves(block)
                acc[...] += dot_nt(jnp.concatenate([high, low], axis=0), ahi[k - 1])
                acc2[...] += dot_nt(high, alo[k - 1])

    def clear():
        acc[...] = jnp.zeros_like(acc)
        acc2[...] = jnp.zeros_like(acc2)

    def e_copy(j, t):
        target = lax.rem(col + t, cols)
        return remote(stage.at[j, target], eland.at[j, t], e_send.at[j, t], e_recv.at[j, t], (row, target))

    def es_copy(j):
        return remote(esend.at[j], esib.at[j], es_send.at[j], es_recv.at[j], (sib, col))

    def scatter(j):
        for i in range(opr):
            mine = pl.multiple_of(i * wpo + j * ROWS, ROWS)
            stage[j, row * opr + i] = eown[pl.ds(mine, ROWS)]
            stage[j, sib * opr + i] = eown[pl.ds(held + mine, ROWS)]
            at_far, at_sib = slice(i * ROWS, (i + 1) * ROWS), slice((opr + i) * ROWS, (opr + i + 1) * ROWS)
            for owner, here in ((far, at_far), (far_sib, at_sib)):
                below = slice(n + here.start, n + here.stop)
                stage[j, owner * opr + i] = acc[here] + (acc[below] + acc2[here])
        loop(1, cols, lambda t: e_copy(j, t).start())

    def gather(j):
        def add(t, total):
            e_copy(j, t).wait_recv()
            return total + eland[j, t]

        esend[j] = lax.fori_loop(1, cols, add, stage[j, col])
        es_copy(j).start()

    def fb_copy(first, last):
        return remote(
            fbs.at[pl.ds(first, last - first)], fbl.at[pl.ds(first, last - first)],
            fb_send.at[first], fb_recv.at[first], (far, col),
        )

    def bias(first, last):
        m = (last - first) * ROWS

        def part(ref):
            high, low = halves(ref[first:last].reshape(m, depth))
            return jnp.concatenate([high, low], axis=0), high

        def term(both, high, q, h):
            here = slice(h * quarter, (h + 1) * quarter)
            pair = dot_nn(both, chi[q, :, here])
            return pair[:m] + (pair[m:] + dot_nn(high, clo[q, :, here]))

        mine = part(esend)
        away, kept = term(*mine, 0, 0), term(*mine, 0, 1)
        for j in range(first, last):
            es_copy(j).wait_recv()
        other = part(esib)
        fbs[first:last] = (away + term(*other, 1, 0)).reshape(last - first, ROWS, quarter)
        fb_copy(first, last).start()
        out[first * ROWS : last * ROWS] = kept + term(*other, 1, 1)

    def turn(j):
        clear()

        @pl.when(j >= slots)
        def _():
            pl.semaphore_wait(s_free, 1)

        steps(j, 0, nkc + 1)
        scatter(j)
        loop(0, nkc, lambda k: f_copy(j, k).wait_send())

        @pl.when(j + slots < ng)
        def _():
            pl.semaphore_signal(x_free, inc=1, device_id=(far, col), device_id_type=MESH)
            pl.semaphore_signal(s_free, inc=1, device_id=(sib, col), device_id_type=MESH)

        @pl.when((j >= 1) & (j + slots - 1 < ng))
        def _():
            pl.semaphore_wait(x_free, 1)

            def again(k):
                x_copy(j - 1, k).wait_send()
                x_copy(j + slots - 1, k).start()

            loop(0, nkc, again)

        for q in range(2):

            @pl.when(j == RELAYS[q])
            def _():
                relay(q)

    last = ng - 1
    if last:
        loop(0, last, turn)
    for q in range(2):
        if RELAYS[q] >= last:
            relay(q)

    for copy in c_copies(0):
        copy.wait_recv()
    for q in range(2):
        loop(1, npeer, lambda p: r_copy(p, q).wait_recv())
    for copy in local:
        copy.wait()
    block = ct.shape[1]

    def c_load(i, slot):
        return pltpu.make_async_copy(cbuf.at[pl.ds(i * block, block)], ct.at[slot], ct_sem.at[slot])

    c_load(0, 0).start()

    @functools.partial(loop, 0, cols // block)
    def _(i):
        slot = lax.rem(i, 2)

        @pl.when(i + 1 < cols // block)
        def _():
            c_load(i + 1, 1 - slot).start()

        c_load(i, slot).wait()
        here = pl.ds(pl.multiple_of(i * block * cr, block * cr), block * cr)
        for q in range(2):
            for h in range(2):
                high, low = halves(ct[slot, :, q, h].reshape(block * cr, quarter))
                chi[q, here, h * quarter : (h + 1) * quarter] = high
                clo[q, here, h * quarter : (h + 1) * quarter] = low

    batches = []
    if last > 1:
        loop(0, last - 1, gather)
        bias(0, last - 1)
        batches.append((0, last - 1))
    clear()
    if last >= slots:
        pl.semaphore_wait(s_free, 1)
    middle = (nkc + 1) // 2
    steps(last, 0, middle)
    if last:
        gather(last - 1)
        bias(last - 1, last)
        batches.append((last - 1, last))
    steps(last, middle, nkc + 1)
    scatter(last)
    gather(last)
    bias(last, ng)
    batches.append((last, ng))
    for first, end in batches:
        fb_copy(first, end).wait_recv()
        out[first * ROWS : end * ROWS] += fbl[first:end].reshape((end - first) * ROWS, quarter)

    loop(0, nkc, lambda k: f_copy(last, k).wait_send())
    for j in range(max(0, ng - slots), ng):
        loop(0, nkc, functools.partial(lambda j, k: x_copy(j, k).wait_send(), j))
    loop(0, nkc, lambda k: n_copy(k).wait_send())
    for copy in to_sib:
        copy.wait_send()

    def sent(p):
        for copy in c_copies(p):
            copy.wait_send()

    loop(0, npeer, sent)
    for q in range(2):
        loop(1, npeer, lambda p: r_copy(p, q).wait_send())

    def e_sent(j):
        loop(1, cols, lambda t: e_copy(j, t).wait_send())
        es_copy(j).wait_send()

    loop(0, ng, e_sent)
    for first, end in batches:
        fb_copy(first, end).wait_send()


def per_device(green_vectors, amplitudes, cholesky):
    rows, cols = lax.axis_size("row"), lax.axis_size("col")
    held, pairs = green_vectors.shape
    depth = amplitudes.shape[0]
    cr, quarter = cholesky.shape[0], cholesky.shape[1] // rows
    if rows != 4 or cols % 2 or rows * held % (cols * ROWS):
        raise ValueError("unexpected mesh")
    wpo = rows * held // cols
    opr, ng = held // wpo, wpo // ROWS
    chunk = min(CHUNK, pairs)
    nkc, nk = pairs // chunk, 2
    slots = min(SLOTS, ng)
    n = 2 * opr * ROWS
    block = max(1, 16 // cr)
    dma = pltpu.SemaphoreType.DMA
    vmem = pltpu.VMEM
    scratch = [
        vmem((nkc, depth, chunk), BF16),
        vmem((nkc, depth, chunk), BF16),
        vmem((2, cols * cr, 2 * quarter), BF16),
        vmem((2, cols * cr, 2 * quarter), BF16),
        vmem((slots, opr, ROWS, pairs), F32),
        vmem((slots, opr, ROWS, pairs), F32),
        vmem((2, depth, TILE), F32),
        vmem((2, 2, opr, ng, ROWS, TILE), F32),
        vmem((2, block, 2, 2, cr, quarter), F32),
        vmem((2 * held, depth), F32),
        vmem((2 * n, depth), F32),
        vmem((n, depth), F32),
        vmem((ng, cols, ROWS, depth), F32),
        vmem((ng, cols, ROWS, depth), F32),
        vmem((ng, ROWS, depth), F32),
        vmem((ng, ROWS, depth), F32),
        vmem((ng, ROWS, quarter), F32),
        vmem((ng, ROWS, quarter), F32),
        dma((slots, nkc)),
        dma((slots, nkc)),
        dma((slots, nkc)),
        dma((slots, nkc)),
        pltpu.SemaphoreType.REGULAR,
        pltpu.SemaphoreType.REGULAR,
        dma((nkc,)),
        dma((nkc,)),
        dma((2, 3)),
        dma((2,)),
        dma((2,)),
        dma((2,)),
        dma((cols // 2, 3)),
        dma((cols // 2, 3)),
        dma((cols // 2, 2)),
        dma((cols // 2, 2)),
        dma((2,)),
        dma((ng, cols)),
        dma((ng, cols)),
        dma((ng,)),
        dma((ng,)),
        dma((ng,)),
        dma((ng,)),
    ]
    hbm = pl.BlockSpec(memory_space=pl.ANY)
    return pl.pallas_call(
        functools.partial(kernel, rows, cols),
        out_shape=(
            jax.ShapeDtypeStruct((wpo, quarter), F32),
            jax.ShapeDtypeStruct((opr, ng, ROWS, pairs), F32),
            jax.ShapeDtypeStruct((cols, 2, 2, cr, quarter), F32),
        ),
        in_specs=[hbm] * 3,
        out_specs=(pl.BlockSpec(memory_space=pltpu.VMEM), hbm, hbm),
        scratch_shapes=scratch,
        compiler_params=pltpu.CompilerParams(
            collective_id=0, has_side_effects=True, vmem_limit_bytes=67_043_328
        ),
    )(green_vectors.reshape(opr, ng, ROWS, pairs), amplitudes, cholesky)[0]


def solution(mesh):
    placed = (P("row", "col"), P("row", "col"), P(("row", "col"), None))
    return jax.shard_map(
        per_device, mesh=mesh, in_specs=placed, out_specs=P("col", "row"), check_vma=False
    )
```

```python
import functools

import jax
import jax.numpy as jnp
from jax import lax
from jax.experimental import pallas as pl
from jax.experimental.pallas import tpu as pltpu
from jax.sharding import PartitionSpec as P

MESH = pl.DeviceIdType.MESH
F32, BF16 = jnp.float32, jnp.bfloat16
ROWS = 8
LATE = 2
SLOTS = 4
CHUNK = 2048
WIDE = 4
TILE = 512
RELAYS = (1, 3)


def halves(x):
    high = x.astype(BF16)
    return high, (x - high.astype(F32)).astype(BF16)


def dot_nt(left, right):
    return lax.dot_general(left, right, (((1,), (1,)), ((), ())), preferred_element_type=F32)


def dot_nn(left, right):
    return jnp.dot(left, right, preferred_element_type=F32)


def kernel(
    rows, cols, g, a, c, out, near, cbuf,
    ahi, alo, chi, clo, xs, ss, at, gt, ct, eown, acc, acc2, stage, eland, esend, esib, fbs, fbl,
    x_send, x_recv, f_send, f_recv, x_free, s_free, up, down, across, n_send, n_recv, ld,
    cl_sem, cs_send, cs_recv, c_send, c_recv, r_send, r_recv, ct_sem,
    e_send, e_recv, es_send, es_recv, fb_send, fb_recv,
):
    row, col = lax.axis_index("row"), lax.axis_index("col")
    sib = row + 1 - 2 * lax.rem(row, 2)
    far = lax.rem(row + rows // 2, rows)
    far_sib = lax.rem(sib + rows // 2, rows)
    pal = col + 1 - 2 * lax.rem(col, 2)
    opr, ng, _, pairs = g.shape
    depth = a.shape[0]
    held, wpo = opr * ng * ROWS, ng * ROWS
    chunk, nkc = ahi.shape[2], ahi.shape[0]
    tile = at.shape[2]
    per = chunk // tile
    cr, quarter = c.shape[0], c.shape[1] // rows
    npeer = cols // 2
    slots = xs.shape[0]
    n = 2 * opr * ROWS

    def remote(src, dst, send, recv, target):
        return pltpu.make_async_remote_copy(
            src_ref=src, dst_ref=dst, send_sem=send, recv_sem=recv, device_id=target, device_id_type=MESH
        )

    def loop(lo, hi, body):
        def step(i, carry):
            body(i)
            return carry

        lax.fori_loop(lo, hi, step, 0)

    barrier = pltpu.get_barrier_semaphore()
    place, places = col // 2, cols // 2
    below, above = place > 0, place < places - 1

    def signal(semaphore, to_row, to_col):
        pl.semaphore_signal(semaphore, inc=1, device_id=(to_row, to_col), device_id_type=MESH)

    signal(barrier, far, col)
    signal(barrier, sib, col)
    signal(barrier, row, pal)
    pl.when(below)(lambda: signal(barrier, row, col - 2))
    pl.when(above)(lambda: signal(barrier, row, col + 2))

    def load(i, slot):
        at_pairs = pl.ds(pl.multiple_of(i * tile, tile), tile)
        return [
            pltpu.make_async_copy(a.at[:, at_pairs], at.at[slot], ld.at[slot, 0]),
            pltpu.make_async_copy(g.at[:, :, :, at_pairs], gt.at[slot, 0], ld.at[slot, 1]),
            pltpu.make_async_copy(near.at[:, :, :, at_pairs], gt.at[slot, 1], ld.at[slot, 2]),
        ]

    for copy in load(0, 0)[:2]:
        copy.start()
    local = [
        pltpu.make_async_copy(
            c.at[:, pl.ds(pl.multiple_of(quarter_of * quarter, quarter), quarter)], cbuf.at[col, 0, h], cl_sem.at[h]
        )
        for h, quarter_of in enumerate((far, row))
    ]
    pl.semaphore_wait(barrier, 3 + jnp.where(below, 1, 0) + jnp.where(above, 1, 0))

    def pairs_of(k):
        return pl.ds(pl.multiple_of(k * chunk, chunk), chunk)

    last = ng - 1
    early = max(0, ng - LATE)
    wide = min(WIDE, nkc)
    half = chunk // 2

    def cut(kind, k):
        if kind == "wide":
            return pl.ds(pl.multiple_of(k * wide * chunk, wide * chunk), wide * chunk)
        if kind == "half":
            return pl.ds(pl.multiple_of((nkc - 1) * chunk + (k - nkc + 1) * half, half), half)
        return pairs_of(k)

    def x_copy(j, k, kind="chunk"):
        slot, here = lax.rem(j, slots), cut(kind, k)
        return remote(
            g.at[:, j, :, here], xs.at[slot, :, :, here], x_send.at[slot, k], x_recv.at[slot, k], (far, col)
        )

    def f_copy(j, k, kind="chunk"):
        slot, here = lax.rem(j, slots), cut(kind, k)
        return remote(
            xs.at[slot, :, :, here], ss.at[slot, :, :, here], f_send.at[slot, k], f_recv.at[slot, k], (sib, col)
        )

    def each(j, body):
        if isinstance(j, int) and j == last:
            loop(0, nkc - 1, lambda k: body(k, "chunk"))
            body(nkc - 1, "half")
            body(nkc, "half")
        elif isinstance(j, int) and j >= early:
            loop(0, nkc, lambda k: body(k, "chunk"))
        else:
            loop(0, nkc // wide, lambda k: body(k, "wide"))

    def start_far(j):
        each(j, lambda k, kind: x_copy(j, k, kind).start())

    def n_copy(k):
        return remote(g.at[:, :, :, pairs_of(k)], near.at[:, :, :, pairs_of(k)], n_send.at[k], n_recv.at[k], (sib, col))

    start_far(0)
    n_copy(0).start()

    def c_quarter(m):
        return c.at[:, pl.ds(pl.multiple_of(m * quarter, quarter), quarter)]

    to_sib = [
        remote(c_quarter(m), cbuf.at[col, 1, h], cs_send.at[h], cs_recv.at[h], (sib, col))
        for h, m in enumerate((far_sib, sib))
    ]

    def c_target(p):
        return jnp.where(p == 0, pal, lax.rem(col + 2 * p, cols))

    def c_source(p):
        return jnp.where(p == 0, pal, lax.rem(col + cols - 2 * p, cols))

    def c_copies(p):
        target = (row, c_target(p))
        return [
            remote(c_quarter(far), cbuf.at[col, 0, 0], c_send.at[p, 0], c_recv.at[p, 0], target),
            remote(c_quarter(row), cbuf.at[col, 0, 1], c_send.at[p, 1], c_recv.at[p, 1], target),
            remote(cbuf.at[col, 1], cbuf.at[col, 1], c_send.at[p, 2], c_recv.at[p, 2], target),
        ]

    def r_copy(p, q):
        piece = cbuf.at[c_source(p), q]
        return remote(piece, piece, r_send.at[p, q], r_recv.at[p, q], (row, pal))

    for copy in to_sib:
        copy.start()
    loop(1, nkc, lambda k: n_copy(k).start())

    def send_own(p):
        for copy in c_copies(p)[:2]:
            copy.start()

    for j in range(1, min(slots, ng)):
        start_far(j)
    for copy in local:
        copy.start()

    @pl.when(below)
    def _():
        pl.semaphore_wait(up, 1)

    pl.when(above)(lambda: signal(up, row, col + 2))

    @pl.when(above)
    def _():
        pl.semaphore_wait(down, 1)

    pl.when(below)(lambda: signal(down, row, col - 2))
    signal(across, row, pal)
    pl.semaphore_wait(across, 1)
    loop(0, npeer, send_own)
    for copy in to_sib:
        copy.wait_recv()
    loop(0, npeer, lambda p: c_copies(p)[2].start())

    def relay(q):
        def one(p):
            copies = c_copies(p)
            for copy in copies[2:] if q else copies[:2]:
                copy.wait_recv()
            r_copy(p, q).start()

        loop(1, npeer, one)

    eown[...] = jnp.zeros_like(eown)
    n_copy(0).wait_recv()
    load(0, 0)[2].start()

    @functools.partial(loop, 0, nkc)
    def _(kk):
        for q in range(per):
            slot = q % 2
            i = kk * per + q
            if q + 1 < per:
                for copy in load(i + 1, 1 - slot):
                    copy.start()
            else:

                @pl.when(kk + 1 < nkc)
                def _():
                    n_copy(kk + 1).wait_recv()
                    for copy in load(i + 1, 1 - slot):
                        copy.start()

            for copy in load(i, slot):
                copy.wait()
            high, low = halves(at[slot])
            ahi[kk, :, q * tile : (q + 1) * tile] = high
            alo[kk, :, q * tile : (q + 1) * tile] = low
            g_high, g_low = halves(gt[slot].reshape(2 * held, tile))
            pair = dot_nt(jnp.concatenate([g_high, g_low], axis=0), high)
            eown[...] += pair[: 2 * held] + (pair[2 * held :] + dot_nt(g_high, low))

    def arrive(j, k, kind):
        x_copy(j, k, kind).wait_recv()
        f_copy(j, k, kind).start()

    def multiply(j, here, left, low_left):
        slot, size = lax.rem(j, slots), left.shape[1]
        block = jnp.concatenate(
            [xs[slot, :, :, here].reshape(n // 2, size), ss[slot, :, :, here].reshape(n // 2, size)], axis=0
        )
        high, low = halves(block)
        acc[...] += dot_nt(jnp.concatenate([high, low], axis=0), left)
        acc2[...] += dot_nt(high, low_left)

    def consume(j, k, kind):
        f_copy(j, k, kind).wait_recv()
        if kind == "wide":
            loop(k * wide, (k + 1) * wide, lambda b: multiply(j, pairs_of(b), ahi[b], alo[b]))
        elif kind == "half":
            here = slice((k - nkc + 1) * half, (k - nkc + 2) * half)
            multiply(j, cut(kind, k), ahi[nkc - 1, :, here], alo[nkc - 1, :, here])
        else:
            multiply(j, pairs_of(k), ahi[k], alo[k])

    def steps(j, lo, hi):
        @functools.partial(loop, lo, hi)
        def _(k):
            arrive(j, k, "chunk")

            @pl.when(k > 0)
            def _():
                consume(j, k - 1, "chunk")

    def clear():
        acc[...] = jnp.zeros_like(acc)
        acc2[...] = jnp.zeros_like(acc2)

    def e_copy(j, t):
        target = lax.rem(col + t, cols)
        return remote(stage.at[j, target], eland.at[j, t], e_send.at[j, t], e_recv.at[j, t], (row, target))

    def es_copy(j):
        return remote(esend.at[j], esib.at[j], es_send.at[j], es_recv.at[j], (sib, col))

    def scatter(j):
        for i in range(opr):
            mine = pl.multiple_of(i * wpo + j * ROWS, ROWS)
            stage[j, row * opr + i] = eown[pl.ds(mine, ROWS)]
            stage[j, sib * opr + i] = eown[pl.ds(held + mine, ROWS)]
            at_far, at_sib = slice(i * ROWS, (i + 1) * ROWS), slice((opr + i) * ROWS, (opr + i + 1) * ROWS)
            for owner, here in ((far, at_far), (far_sib, at_sib)):
                below = slice(n + here.start, n + here.stop)
                stage[j, owner * opr + i] = acc[here] + (acc[below] + acc2[here])
        loop(1, cols, lambda t: e_copy(j, t).start())

    def gather(j):
        def add(t, total):
            e_copy(j, t).wait_recv()
            return total + eland[j, t]

        esend[j] = lax.fori_loop(1, cols, add, stage[j, col])
        es_copy(j).start()

    def fb_copy(first, last):
        return remote(
            fbs.at[pl.ds(first, last - first)], fbl.at[pl.ds(first, last - first)],
            fb_send.at[first], fb_recv.at[first], (far, col),
        )

    def bias(first, last):
        m = (last - first) * ROWS

        def part(ref):
            high, low = halves(ref[first:last].reshape(m, depth))
            return jnp.concatenate([high, low], axis=0), high

        def term(both, high, q, h):
            here = slice(h * quarter, (h + 1) * quarter)
            pair = dot_nn(both, chi[q, :, here])
            return pair[:m] + (pair[m:] + dot_nn(high, clo[q, :, here]))

        mine = part(esend)
        away, kept = term(*mine, 0, 0), term(*mine, 0, 1)
        for j in range(first, last):
            es_copy(j).wait_recv()
        other = part(esib)
        fbs[first:last] = (away + term(*other, 1, 0)).reshape(last - first, ROWS, quarter)
        fb_copy(first, last).start()
        out[first * ROWS : last * ROWS] = kept + term(*other, 1, 1)

    def pass_on(j):
        for q in range(2):

            @pl.when(j == RELAYS[q])
            def _():
                relay(q)

    def turn(j):
        clear()

        @pl.when(j >= slots)
        def _():
            pl.semaphore_wait(s_free, 1)

        def one(k):
            arrive(j, k, "wide")
            consume(j, k, "wide")

        loop(0, nkc // wide, one)
        scatter(j)
        each(j, lambda k, kind: f_copy(j, k, kind).wait_send())

        @pl.when(j + slots < ng)
        def _():
            signal(x_free, far, col)
            signal(s_free, sib, col)

        later = j + slots - 1

        @pl.when((j >= 1) & (later < ng))
        def _():
            pl.semaphore_wait(x_free, 1)
            each(j, lambda k, kind: x_copy(j - 1, k, kind).wait_send())
            pl.when(later < early)(lambda: start_far(later))
            for m in range(max(slots, early), ng):
                pl.when(later == m)(functools.partial(start_far, m))

        pass_on(j)

    loop(0, early, turn)
    for q in range(2):
        if RELAYS[q] >= early:
            relay(q)

    for copy in c_copies(0):
        copy.wait_recv()
    for q in range(2):
        loop(1, npeer, lambda p: r_copy(p, q).wait_recv())
    for copy in local:
        copy.wait()
    block = ct.shape[1]

    def c_load(i, slot):
        return pltpu.make_async_copy(cbuf.at[pl.ds(i * block, block)], ct.at[slot], ct_sem.at[slot])

    c_load(0, 0).start()

    @functools.partial(loop, 0, cols // block)
    def _(i):
        slot = lax.rem(i, 2)

        @pl.when(i + 1 < cols // block)
        def _():
            c_load(i + 1, 1 - slot).start()

        c_load(i, slot).wait()
        here = pl.ds(pl.multiple_of(i * block * cr, block * cr), block * cr)
        for q in range(2):
            for h in range(2):
                high, low = halves(ct[slot, :, q, h].reshape(block * cr, quarter))
                chi[q, here, h * quarter : (h + 1) * quarter] = high
                clo[q, here, h * quarter : (h + 1) * quarter] = low

    batches = []

    def finish(end):
        first = batches[-1][1] if batches else 0
        if first < end:
            loop(first, end, gather)
            bias(first, end)
            batches.append((first, end))

    finish(early - 1)
    for j in range(early, ng):
        clear()
        if j >= slots:
            pl.semaphore_wait(s_free, 1)
        if j < last:
            steps(j, 0, nkc)
            consume(j, nkc - 1, "chunk")
        else:
            middle = (nkc - 1) // 2
            steps(j, 0, middle)
            finish(last)
            steps(j, middle, nkc - 1)
            arrive(j, nkc - 1, "half")
            if nkc > 1:
                consume(j, nkc - 2, "chunk")
            arrive(j, nkc, "half")
            consume(j, nkc - 1, "half")
            consume(j, nkc, "half")
        scatter(j)
        if j < last:
            each(j, functools.partial(lambda j, k, kind: f_copy(j, k, kind).wait_send(), j))
    finish(ng)
    for first, end in batches:
        fb_copy(first, end).wait_recv()
        out[first * ROWS : end * ROWS] += fbl[first:end].reshape((end - first) * ROWS, quarter)

    each(last, lambda k, kind: f_copy(last, k, kind).wait_send())
    for j in range(max(0, ng - slots), ng):
        each(j, functools.partial(lambda j, k, kind: x_copy(j, k, kind).wait_send(), j))
    loop(0, nkc, lambda k: n_copy(k).wait_send())
    for copy in to_sib:
        copy.wait_send()

    def sent(p):
        for copy in c_copies(p):
            copy.wait_send()

    loop(0, npeer, sent)
    for q in range(2):
        loop(1, npeer, lambda p: r_copy(p, q).wait_send())

    def e_sent(j):
        loop(1, cols, lambda t: e_copy(j, t).wait_send())
        es_copy(j).wait_send()

    loop(0, ng, e_sent)
    for first, end in batches:
        fb_copy(first, end).wait_send()


def per_device(green_vectors, amplitudes, cholesky):
    rows, cols = lax.axis_size("row"), lax.axis_size("col")
    held, pairs = green_vectors.shape
    depth = amplitudes.shape[0]
    cr, quarter = cholesky.shape[0], cholesky.shape[1] // rows
    if rows != 4 or cols % 2 or rows * held % (cols * ROWS):
        raise ValueError("unexpected mesh")
    wpo = rows * held // cols
    opr, ng = held // wpo, wpo // ROWS
    chunk = min(CHUNK, pairs)
    nkc, nk = pairs // chunk, 2
    slots = min(SLOTS, ng)
    n = 2 * opr * ROWS
    block = max(1, 16 // cr)
    dma = pltpu.SemaphoreType.DMA
    vmem = pltpu.VMEM
    scratch = [
        vmem((nkc, depth, chunk), BF16),
        vmem((nkc, depth, chunk), BF16),
        vmem((2, cols * cr, 2 * quarter), BF16),
        vmem((2, cols * cr, 2 * quarter), BF16),
        vmem((slots, opr, ROWS, pairs), F32),
        vmem((slots, opr, ROWS, pairs), F32),
        vmem((2, depth, TILE), F32),
        vmem((2, 2, opr, ng, ROWS, TILE), F32),
        vmem((2, block, 2, 2, cr, quarter), F32),
        vmem((2 * held, depth), F32),
        vmem((2 * n, depth), F32),
        vmem((n, depth), F32),
        vmem((ng, cols, ROWS, depth), F32),
        vmem((ng, cols, ROWS, depth), F32),
        vmem((ng, ROWS, depth), F32),
        vmem((ng, ROWS, depth), F32),
        vmem((ng, ROWS, quarter), F32),
        vmem((ng, ROWS, quarter), F32),
        dma((slots, nkc + 1)),
        dma((slots, nkc + 1)),
        dma((slots, nkc + 1)),
        dma((slots, nkc + 1)),
        *[pltpu.SemaphoreType.REGULAR] * 5,
        dma((nkc,)),
        dma((nkc,)),
        dma((2, 3)),
        dma((2,)),
        dma((2,)),
        dma((2,)),
        dma((cols // 2, 3)),
        dma((cols // 2, 3)),
        dma((cols // 2, 2)),
        dma((cols // 2, 2)),
        dma((2,)),
        dma((ng, cols)),
        dma((ng, cols)),
        dma((ng,)),
        dma((ng,)),
        dma((ng,)),
        dma((ng,)),
    ]
    hbm = pl.BlockSpec(memory_space=pl.ANY)
    return pl.pallas_call(
        functools.partial(kernel, rows, cols),
        out_shape=(
            jax.ShapeDtypeStruct((wpo, quarter), F32),
            jax.ShapeDtypeStruct((opr, ng, ROWS, pairs), F32),
            jax.ShapeDtypeStruct((cols, 2, 2, cr, quarter), F32),
        ),
        in_specs=[hbm] * 3,
        out_specs=(pl.BlockSpec(memory_space=pltpu.VMEM), hbm, hbm),
        scratch_shapes=scratch,
        compiler_params=pltpu.CompilerParams(
            collective_id=0, has_side_effects=True, vmem_limit_bytes=67_043_328
        ),
    )(green_vectors.reshape(opr, ng, ROWS, pairs), amplitudes, cholesky)[0]


def solution(mesh):
    placed = (P("row", "col"), P("row", "col"), P(("row", "col"), None))
    return jax.shard_map(
        per_device, mesh=mesh, in_specs=placed, out_specs=P("col", "row"), check_vma=False
    )
```

```python
import functools

import jax
import jax.numpy as jnp
from jax import lax
from jax.experimental import pallas as pl
from jax.experimental.pallas import tpu as pltpu
from jax.sharding import PartitionSpec as P

MESH = pl.DeviceIdType.MESH
F32, BF16 = jnp.float32, jnp.bfloat16
ROWS = 8
LATE = 2
SLOTS = 4
CHUNK = 2048
WIDE = 2
TILE = 512
RELAYS = (1, 3)


def halves(x):
    high = x.astype(BF16)
    return high, (x - high.astype(F32)).astype(BF16)


def dot_nt(left, right):
    return lax.dot_general(left, right, (((1,), (1,)), ((), ())), preferred_element_type=F32)


def dot_nn(left, right):
    return jnp.dot(left, right, preferred_element_type=F32)


def kernel(
    rows, cols, g, a, c, out, near, cbuf,
    ahi, alo, chi, clo, xs, ss, at, gt, ct, eown, acc, acc2, stage, eland, esend, esib, fbs, fbl,
    x_send, x_recv, f_send, f_recv, x_free, s_free, up, down, across, n_send, n_recv, ld,
    cl_sem, cs_send, cs_recv, c_send, c_recv, r_send, r_recv, ct_sem,
    e_send, e_recv, es_send, es_recv, fb_send, fb_recv,
):
    row, col = lax.axis_index("row"), lax.axis_index("col")
    sib = row + 1 - 2 * lax.rem(row, 2)
    far = lax.rem(row + rows // 2, rows)
    far_sib = lax.rem(sib + rows // 2, rows)
    pal = col + 1 - 2 * lax.rem(col, 2)
    opr, ng, _, pairs = g.shape
    depth = a.shape[0]
    held, wpo = opr * ng * ROWS, ng * ROWS
    chunk, nkc = ahi.shape[2], ahi.shape[0]
    tile = at.shape[2]
    per = chunk // tile
    cr, quarter = c.shape[0], c.shape[1] // rows
    npeer = cols // 2
    slots = xs.shape[0]
    n = 2 * opr * ROWS

    def remote(src, dst, send, recv, target):
        return pltpu.make_async_remote_copy(
            src_ref=src, dst_ref=dst, send_sem=send, recv_sem=recv, device_id=target, device_id_type=MESH
        )

    def loop(lo, hi, body):
        def step(i, carry):
            body(i)
            return carry

        lax.fori_loop(lo, hi, step, 0)

    barrier = pltpu.get_barrier_semaphore()
    place, places = col // 2, cols // 2
    below, above = place > 0, place < places - 1

    def signal(semaphore, to_row, to_col):
        pl.semaphore_signal(semaphore, inc=1, device_id=(to_row, to_col), device_id_type=MESH)

    signal(barrier, far, col)
    signal(barrier, sib, col)
    signal(barrier, row, pal)
    pl.when(below)(lambda: signal(barrier, row, col - 2))
    pl.when(above)(lambda: signal(barrier, row, col + 2))

    def load(i, slot):
        at_pairs = pl.ds(pl.multiple_of(i * tile, tile), tile)
        return [
            pltpu.make_async_copy(a.at[:, at_pairs], at.at[slot], ld.at[slot, 0]),
            pltpu.make_async_copy(g.at[:, :, :, at_pairs], gt.at[slot, 0], ld.at[slot, 1]),
            pltpu.make_async_copy(near.at[:, :, :, at_pairs], gt.at[slot, 1], ld.at[slot, 2]),
        ]

    for copy in load(0, 0)[:2]:
        copy.start()
    local = [
        pltpu.make_async_copy(
            c.at[:, pl.ds(pl.multiple_of(quarter_of * quarter, quarter), quarter)], cbuf.at[col, 0, h], cl_sem.at[h]
        )
        for h, quarter_of in enumerate((far, row))
    ]
    pl.semaphore_wait(barrier, 3 + jnp.where(below, 1, 0) + jnp.where(above, 1, 0))

    def pairs_of(k):
        return pl.ds(pl.multiple_of(k * chunk, chunk), chunk)

    last = ng - 1
    early = max(0, ng - LATE)
    wide = min(WIDE, nkc)
    half = chunk // 2

    def cut(kind, k):
        if kind == "wide":
            return pl.ds(pl.multiple_of(k * wide * chunk, wide * chunk), wide * chunk)
        if kind == "half":
            return pl.ds(pl.multiple_of((nkc - 1) * chunk + (k - nkc + 1) * half, half), half)
        return pairs_of(k)

    def x_copy(j, k, kind="chunk"):
        slot, here = lax.rem(j, slots), cut(kind, k)
        return remote(
            g.at[:, j, :, here], xs.at[slot, :, :, here], x_send.at[slot, k], x_recv.at[slot, k], (far, col)
        )

    def f_copy(j, k, kind="chunk"):
        slot, here = lax.rem(j, slots), cut(kind, k)
        return remote(
            xs.at[slot, :, :, here], ss.at[slot, :, :, here], f_send.at[slot, k], f_recv.at[slot, k], (sib, col)
        )

    def each(j, body):
        if isinstance(j, int) and j == last:
            loop(0, nkc - 1, lambda k: body(k, "chunk"))
            body(nkc - 1, "half")
            body(nkc, "half")
        elif isinstance(j, int) and j >= early:
            loop(0, nkc, lambda k: body(k, "chunk"))
        else:
            loop(0, nkc // wide, lambda k: body(k, "wide"))

    def start_far(j):
        each(j, lambda k, kind: x_copy(j, k, kind).start())

    def n_copy(k):
        return remote(g.at[:, :, :, pairs_of(k)], near.at[:, :, :, pairs_of(k)], n_send.at[k], n_recv.at[k], (sib, col))

    start_far(0)
    n_copy(0).start()

    def c_quarter(m):
        return c.at[:, pl.ds(pl.multiple_of(m * quarter, quarter), quarter)]

    to_sib = [
        remote(c_quarter(m), cbuf.at[col, 1, h], cs_send.at[h], cs_recv.at[h], (sib, col))
        for h, m in enumerate((far_sib, sib))
    ]

    def c_target(p):
        return jnp.where(p == 0, pal, lax.rem(col + 2 * p, cols))

    def c_source(p):
        return jnp.where(p == 0, pal, lax.rem(col + cols - 2 * p, cols))

    def c_copies(p):
        target = (row, c_target(p))
        return [
            remote(c_quarter(far), cbuf.at[col, 0, 0], c_send.at[p, 0], c_recv.at[p, 0], target),
            remote(c_quarter(row), cbuf.at[col, 0, 1], c_send.at[p, 1], c_recv.at[p, 1], target),
            remote(cbuf.at[col, 1], cbuf.at[col, 1], c_send.at[p, 2], c_recv.at[p, 2], target),
        ]

    def r_copy(p, q):
        piece = cbuf.at[c_source(p), q]
        return remote(piece, piece, r_send.at[p, q], r_recv.at[p, q], (row, pal))

    for copy in to_sib:
        copy.start()
    loop(1, nkc, lambda k: n_copy(k).start())

    def send_own(p):
        for copy in c_copies(p)[:2]:
            copy.start()

    for j in range(1, min(slots, ng)):
        start_far(j)
    for copy in local:
        copy.start()

    @pl.when(below)
    def _():
        pl.semaphore_wait(up, 1)

    pl.when(above)(lambda: signal(up, row, col + 2))

    @pl.when(above)
    def _():
        pl.semaphore_wait(down, 1)

    pl.when(below)(lambda: signal(down, row, col - 2))
    signal(across, row, pal)
    pl.semaphore_wait(across, 1)
    loop(0, npeer, send_own)
    for copy in to_sib:
        copy.wait_recv()
    loop(0, npeer, lambda p: c_copies(p)[2].start())

    def relay(q):
        def one(p):
            copies = c_copies(p)
            for copy in copies[2:] if q else copies[:2]:
                copy.wait_recv()
            r_copy(p, q).start()

        loop(1, npeer, one)

    eown[...] = jnp.zeros_like(eown)
    n_copy(0).wait_recv()
    load(0, 0)[2].start()

    @functools.partial(loop, 0, nkc)
    def _(kk):
        for q in range(per):
            slot = q % 2
            i = kk * per + q
            if q + 1 < per:
                for copy in load(i + 1, 1 - slot):
                    copy.start()
            else:

                @pl.when(kk + 1 < nkc)
                def _():
                    n_copy(kk + 1).wait_recv()
                    for copy in load(i + 1, 1 - slot):
                        copy.start()

            for copy in load(i, slot):
                copy.wait()
            high, low = halves(at[slot])
            ahi[kk, :, q * tile : (q + 1) * tile] = high
            alo[kk, :, q * tile : (q + 1) * tile] = low
            g_high, g_low = halves(gt[slot].reshape(2 * held, tile))
            pair = dot_nt(jnp.concatenate([g_high, g_low], axis=0), high)
            eown[...] += pair[: 2 * held] + (pair[2 * held :] + dot_nt(g_high, low))

    def arrive(j, k, kind):
        x_copy(j, k, kind).wait_recv()
        f_copy(j, k, kind).start()

    def multiply(j, here, left, low_left):
        slot, size = lax.rem(j, slots), left.shape[1]
        block = jnp.concatenate(
            [xs[slot, :, :, here].reshape(n // 2, size), ss[slot, :, :, here].reshape(n // 2, size)], axis=0
        )
        high, low = halves(block)
        acc[...] += dot_nt(jnp.concatenate([high, low], axis=0), left)
        acc2[...] += dot_nt(high, low_left)

    def consume(j, k, kind):
        f_copy(j, k, kind).wait_recv()
        if kind == "wide":
            loop(k * wide, (k + 1) * wide, lambda b: multiply(j, pairs_of(b), ahi[b], alo[b]))
        elif kind == "half":
            here = slice((k - nkc + 1) * half, (k - nkc + 2) * half)
            multiply(j, cut(kind, k), ahi[nkc - 1, :, here], alo[nkc - 1, :, here])
        else:
            multiply(j, pairs_of(k), ahi[k], alo[k])

    def steps(j, lo, hi):
        @functools.partial(loop, lo, hi)
        def _(k):
            arrive(j, k, "chunk")

            @pl.when(k > 0)
            def _():
                consume(j, k - 1, "chunk")

    def clear():
        acc[...] = jnp.zeros_like(acc)
        acc2[...] = jnp.zeros_like(acc2)

    def e_copy(j, t):
        target = lax.rem(col + t, cols)
        return remote(stage.at[j, target], eland.at[j, t], e_send.at[j, t], e_recv.at[j, t], (row, target))

    def es_copy(j):
        return remote(esend.at[j], esib.at[j], es_send.at[j], es_recv.at[j], (sib, col))

    def send(j, here):
        def one(t):
            owner = lax.rem(col + t, cols) // opr
            pl.when((owner // 2 == row // 2) == here)(lambda: e_copy(j, t).start())

        loop(1, cols, one)

    def scatter_own(j):
        for i in range(opr):
            mine = pl.multiple_of(i * wpo + j * ROWS, ROWS)
            stage[j, row * opr + i] = eown[pl.ds(mine, ROWS)]
            stage[j, sib * opr + i] = eown[pl.ds(held + mine, ROWS)]
        send(j, True)

    def scatter_far(j):
        for i in range(opr):
            at_far, at_sib = slice(i * ROWS, (i + 1) * ROWS), slice((opr + i) * ROWS, (opr + i + 1) * ROWS)
            for owner, here in ((far, at_far), (far_sib, at_sib)):
                below = slice(n + here.start, n + here.stop)
                stage[j, owner * opr + i] = acc[here] + (acc[below] + acc2[here])
        send(j, False)

    def gather(j):
        def add(t, total):
            e_copy(j, t).wait_recv()
            return total + eland[j, t]

        esend[j] = lax.fori_loop(1, cols, add, stage[j, col])
        es_copy(j).start()

    def fb_copy(first, last):
        return remote(
            fbs.at[pl.ds(first, last - first)], fbl.at[pl.ds(first, last - first)],
            fb_send.at[first], fb_recv.at[first], (far, col),
        )

    def bias(first, last):
        m = (last - first) * ROWS

        def part(ref):
            high, low = halves(ref[first:last].reshape(m, depth))
            return jnp.concatenate([high, low], axis=0), high

        def term(both, high, q, h):
            here = slice(h * quarter, (h + 1) * quarter)
            pair = dot_nn(both, chi[q, :, here])
            return pair[:m] + (pair[m:] + dot_nn(high, clo[q, :, here]))

        mine = part(esend)
        away, kept = term(*mine, 0, 0), term(*mine, 0, 1)
        for j in range(first, last):
            es_copy(j).wait_recv()
        other = part(esib)
        fbs[first:last] = (away + term(*other, 1, 0)).reshape(last - first, ROWS, quarter)
        if last == ng:
            fb_copy(first, last).start()
        out[first * ROWS : last * ROWS] = kept + term(*other, 1, 1)

    def pass_on(j):
        for q in range(2):

            @pl.when(j == RELAYS[q])
            def _():
                relay(q)

    def turn(j):
        clear()

        @pl.when(j >= slots)
        def _():
            pl.semaphore_wait(s_free, 1)

        def one(k):
            @pl.when(k < nkc // wide)
            def _():
                arrive(j, k, "wide")

            @pl.when(k > 0)
            def _():
                consume(j, k - 1, "wide")

        loop(0, nkc // wide + 1, one)
        scatter_own(j)
        scatter_far(j)
        each(j, lambda k, kind: f_copy(j, k, kind).wait_send())

        @pl.when(j + slots < ng)
        def _():
            signal(x_free, far, col)
            signal(s_free, sib, col)

        later = j + slots - 1

        @pl.when((j >= 1) & (later < ng))
        def _():
            pl.semaphore_wait(x_free, 1)
            each(j, lambda k, kind: x_copy(j - 1, k, kind).wait_send())
            pl.when(later < early)(lambda: start_far(later))
            for m in range(max(slots, early), ng):
                pl.when(later == m)(functools.partial(start_far, m))

        pass_on(j)

    loop(0, early, turn)
    for q in range(2):
        if RELAYS[q] >= early:
            relay(q)

    for copy in c_copies(0):
        copy.wait_recv()
    for q in range(2):
        loop(1, npeer, lambda p: r_copy(p, q).wait_recv())
    for copy in local:
        copy.wait()
    block = ct.shape[1]

    def c_load(i, slot):
        return pltpu.make_async_copy(cbuf.at[pl.ds(i * block, block)], ct.at[slot], ct_sem.at[slot])

    c_load(0, 0).start()

    @functools.partial(loop, 0, cols // block)
    def _(i):
        slot = lax.rem(i, 2)

        @pl.when(i + 1 < cols // block)
        def _():
            c_load(i + 1, 1 - slot).start()

        c_load(i, slot).wait()
        here = pl.ds(pl.multiple_of(i * block * cr, block * cr), block * cr)
        for q in range(2):
            for h in range(2):
                high, low = halves(ct[slot, :, q, h].reshape(block * cr, quarter))
                chi[q, here, h * quarter : (h + 1) * quarter] = high
                clo[q, here, h * quarter : (h + 1) * quarter] = low

    batches = []

    def finish(end):
        first = batches[-1][1] if batches else 0
        if first < end:
            loop(first, end, gather)
            bias(first, end)
            batches.append((first, end))

    finish(early - 1)
    for j in range(early, ng):
        clear()
        if j >= slots:
            pl.semaphore_wait(s_free, 1)
        if j < last:
            steps(j, 0, nkc)
            consume(j, nkc - 1, "chunk")
        else:
            middle = (nkc - 1) // 2
            steps(j, 0, middle)
            finish(last)
            scatter_own(j)
            steps(j, middle, nkc - 1)
            arrive(j, nkc - 1, "half")
            if nkc > 1:
                consume(j, nkc - 2, "chunk")
            arrive(j, nkc, "half")
            for pair in batches:
                fb_copy(*pair).start()
            consume(j, nkc - 1, "half")
            consume(j, nkc, "half")
        if j < last:
            scatter_own(j)
        scatter_far(j)
        if j < last:
            each(j, functools.partial(lambda j, k, kind: f_copy(j, k, kind).wait_send(), j))
    finish(ng)
    for first, end in batches:
        fb_copy(first, end).wait_recv()
        out[first * ROWS : end * ROWS] += fbl[first:end].reshape((end - first) * ROWS, quarter)

    each(last, lambda k, kind: f_copy(last, k, kind).wait_send())
    for j in range(max(0, ng - slots), ng):
        each(j, functools.partial(lambda j, k, kind: x_copy(j, k, kind).wait_send(), j))
    loop(0, nkc, lambda k: n_copy(k).wait_send())
    for copy in to_sib:
        copy.wait_send()

    def sent(p):
        for copy in c_copies(p):
            copy.wait_send()

    loop(0, npeer, sent)
    for q in range(2):
        loop(1, npeer, lambda p: r_copy(p, q).wait_send())

    def e_sent(j):
        loop(1, cols, lambda t: e_copy(j, t).wait_send())
        es_copy(j).wait_send()

    loop(0, ng, e_sent)
    for first, end in batches:
        fb_copy(first, end).wait_send()


def per_device(green_vectors, amplitudes, cholesky):
    rows, cols = lax.axis_size("row"), lax.axis_size("col")
    held, pairs = green_vectors.shape
    depth = amplitudes.shape[0]
    cr, quarter = cholesky.shape[0], cholesky.shape[1] // rows
    if rows != 4 or cols % 2 or rows * held % (cols * ROWS):
        raise ValueError("unexpected mesh")
    wpo = rows * held // cols
    opr, ng = held // wpo, wpo // ROWS
    chunk = min(CHUNK, pairs)
    nkc, nk = pairs // chunk, 2
    slots = min(SLOTS, ng)
    n = 2 * opr * ROWS
    block = max(1, 16 // cr)
    dma = pltpu.SemaphoreType.DMA
    vmem = pltpu.VMEM
    scratch = [
        vmem((nkc, depth, chunk), BF16),
        vmem((nkc, depth, chunk), BF16),
        vmem((2, cols * cr, 2 * quarter), BF16),
        vmem((2, cols * cr, 2 * quarter), BF16),
        vmem((slots, opr, ROWS, pairs), F32),
        vmem((slots, opr, ROWS, pairs), F32),
        vmem((2, depth, TILE), F32),
        vmem((2, 2, opr, ng, ROWS, TILE), F32),
        vmem((2, block, 2, 2, cr, quarter), F32),
        vmem((2 * held, depth), F32),
        vmem((2 * n, depth), F32),
        vmem((n, depth), F32),
        vmem((ng, cols, ROWS, depth), F32),
        vmem((ng, cols, ROWS, depth), F32),
        vmem((ng, ROWS, depth), F32),
        vmem((ng, ROWS, depth), F32),
        vmem((ng, ROWS, quarter), F32),
        vmem((ng, ROWS, quarter), F32),
        dma((slots, nkc + 1)),
        dma((slots, nkc + 1)),
        dma((slots, nkc + 1)),
        dma((slots, nkc + 1)),
        *[pltpu.SemaphoreType.REGULAR] * 5,
        dma((nkc,)),
        dma((nkc,)),
        dma((2, 3)),
        dma((2,)),
        dma((2,)),
        dma((2,)),
        dma((cols // 2, 3)),
        dma((cols // 2, 3)),
        dma((cols // 2, 2)),
        dma((cols // 2, 2)),
        dma((2,)),
        dma((ng, cols)),
        dma((ng, cols)),
        dma((ng,)),
        dma((ng,)),
        dma((ng,)),
        dma((ng,)),
    ]
    hbm = pl.BlockSpec(memory_space=pl.ANY)
    return pl.pallas_call(
        functools.partial(kernel, rows, cols),
        out_shape=(
            jax.ShapeDtypeStruct((wpo, quarter), F32),
            jax.ShapeDtypeStruct((opr, ng, ROWS, pairs), F32),
            jax.ShapeDtypeStruct((cols, 2, 2, cr, quarter), F32),
        ),
        in_specs=[hbm] * 3,
        out_specs=(pl.BlockSpec(memory_space=pltpu.VMEM), hbm, hbm),
        scratch_shapes=scratch,
        compiler_params=pltpu.CompilerParams(
            collective_id=0, has_side_effects=True, vmem_limit_bytes=67_043_328
        ),
    )(green_vectors.reshape(opr, ng, ROWS, pairs), amplitudes, cholesky)[0]


def solution(mesh):
    placed = (P("row", "col"), P("row", "col"), P(("row", "col"), None))
    return jax.shard_map(
        per_device, mesh=mesh, in_specs=placed, out_specs=P("col", "row"), check_vma=False
    )
```
